32 devices in a mesh: mode: 2 (over x), space: 16 (over z, y, core).
Axes of the slice: x: 2, y: 2, z: 4, core: 2. Of those that a mesh axis runs over, the one named last changes fastest.
Arguments:
- field: bfloat16 [64, 256, 1024], P('mode', 'space'), may hold values from -6 to 6
- kappa_x: float32 [8, 256, 1024], P(None, 'space'), may hold values from -4 to 4
- kappa_y: float32 [8, 256, 1024], P(None, 'space'), may hold values from -4 to 4
- coupling: bfloat16 [4, 8, 32, 32], P('mode'), may hold values from -0.625 to 0.625
- pattern: int32 [4, 8, 32, 32], P('mode'), may hold values 0 or 1
Outputs:
- image: float32 [64, 256, 1024], P('mode', 'space')
The draws below stay inside these ranges and needn't reach their ends.
All inputs are finite; a program needn't handle non-finite values. No bound on the sum of `pattern` on one device may be relied on, other than what follows from the above.
Results may differ from the reference program's by a relative error of at most 0.0003.
Values may be sent and summed in bfloat16 or wider, within the bound.
A program may use at most 64 MiB of HBM per device.

```python
import jax
import jax.numpy as jnp
from jax import lax

MB = 32
K = 8
ROUNDS = 1
NY = 1024
MODES = 64
NX = 256
N_MODE = 2


def place_ends(values, rng, least, high):
    place = [jax.random.randint(jax.random.fold_in(rng, axis), (), 0, length) for axis, length in enumerate(values.shape)]
    main_axis = values.shape.index(max(values.shape))
    beside = place[:main_axis] + [(place[main_axis] + 1) % values.shape[main_axis]] + place[main_axis + 1:]
    return values.at[tuple(place)].set(least).at[tuple(beside)].set(high)


def shard_levels(stream_key, dims, pieces, low, high):
    gain = 1.0
    for axis_at, shards_of in pieces:
        steps = jax.random.uniform(jax.random.fold_in(jax.random.fold_in(stream_key, 6), axis_at), (shards_of,), jnp.float32, low / len(pieces), high / len(pieces))
        gain = gain * jnp.repeat(jnp.exp(steps), dims[axis_at] // shards_of).reshape((-1,) + (1,) * (len(dims) - 1 - axis_at))
    return gain


def gaussian(rng, extent, deviation, limit, shards=(), kind=jnp.bfloat16):
    level = shard_levels(rng, extent, shards, -0.22, 0.18) if shards else 1.0
    values = jax.random.normal(rng, extent, jnp.float32) * deviation * level
    return jnp.minimum(jnp.maximum(values, -limit), limit).astype(kind)


def setup_inputs(seed: int = 0) -> dict:
    seeds = jax.random.split(jax.random.key(seed), 6)
    return {
        "field": gaussian(seeds[0], (MODES, NX, NY), 1.0, 6.0, ((0, 2), (1, 16))),
        "kappa_x": gaussian(seeds[1], (K, NX, NY), 0.5, 4.0, ((1, 16),), jnp.float32),
        "kappa_y": gaussian(seeds[2], (K, NX, NY), 0.5, 4.0, ((1, 16),), jnp.float32),
        "coupling": gaussian(seeds[3], (N_MODE * (ROUNDS + 1), K, MB, MB), (3 * MB) ** -0.5, 0.625, ((0, 2),)),
        "pattern": place_ends((jax.random.randint(seeds[4], (N_MODE * (ROUNDS + 1), K, MB, MB), 0, 3) < 1).astype(jnp.int32), jax.random.fold_in(seeds[4], 1), 0, 1),
    }


def mix(coef_k, block):
    return jnp.einsum("ij,jrw->irw", coef_k, block, precision=lax.Precision.HIGHEST)


def reference(field, kappa_x, kappa_y, coupling, pattern):
    zeros_bf = jnp.zeros(coupling.shape, jnp.bfloat16)
    coef = jnp.where(pattern > 0, coupling, zeros_bf).astype(jnp.float32)
    coef = coef.reshape(N_MODE, ROUNDS + 1, K, MB, MB)
    blocks = field.astype(jnp.float32).reshape(N_MODE, MB, NX, NY)
    padded = jnp.concatenate([blocks, jnp.zeros((N_MODE, MB, 1, NY), jnp.float32)], axis=2)

    def one_block(index):
        own = padded[index]
        flux_x = jnp.zeros((MB, NX, NY), jnp.float32)
        flux_y = jnp.zeros((MB, NX, NY), jnp.float32)
        for k in range(K):
            ck = coef[index, 0, k]
            wk = 0.5 * (mix(ck, own) + mix(ck.T, own))
            for r in range(1, ROUNDS + 1):
                upper = (index + r) % N_MODE
                lower = (index - r) % N_MODE
                wk = wk + mix(coef[index, r, k], padded[upper]) + mix(coef[lower, r, k].T, padded[lower])
            inner = wk[:, :NX, :]
            diff_x = wk[:, 1:, :] - inner
            next_col = jnp.concatenate([inner[:, :, 1:], jnp.zeros((MB, NX, 1), jnp.float32)], axis=2)
            flux_x = flux_x + kappa_x[k] * diff_x
            flux_y = flux_y + kappa_y[k] * (next_col - inner)
        prev_x = jnp.concatenate([jnp.zeros((MB, 1, NY), jnp.float32), flux_x[:, :-1, :]], axis=1)
        prev_y = jnp.concatenate([jnp.zeros((MB, NX, 1), jnp.float32), flux_y[:, :, :-1]], axis=2)
        return -(flux_x - prev_x) - (flux_y - prev_y)

    result = lax.map(one_block, jnp.arange(N_MODE, dtype=jnp.int32))
    return result.reshape(MODES, NX, NY)
```

```python
import functools

import jax
import jax.numpy as jnp
from jax import lax
from jax.experimental import pallas as pl
from jax.experimental.pallas import tpu as pltpu
from jax.sharding import PartitionSpec as P

LANES = 256


def kernel(n_mode, n_space, u_hbm, kx_ref, ky_ref, a_ref, ct_hbm, kx_hbm, out_ref,
           u_ext, v_ext, ct_in, kx_in, fx_prev, fy_row, sh,
           local_sem, main_send, main_recv, halo_send, halo_recv):
    rows, mb, ny = u_hbm.shape
    terms = kx_ref.shape[0]
    sides = v_ext.shape[0]
    mode = lax.axis_index("mode")
    space = lax.axis_index("space")
    above = {"space": lax.rem(space + 1, n_space)}
    below = {"space": lax.rem(space + n_space - 1, n_space)}
    upper = {"mode": lax.rem(mode + 1, n_mode)}
    lower = {"mode": lax.rem(mode + n_mode - 1, n_mode)}

    barrier = pltpu.get_barrier_semaphore()
    for target in (above, below, upper, lower):
        pl.semaphore_signal(barrier, inc=1, device_id=target, device_id_type=pl.DeviceIdType.MESH)
    own = pltpu.make_async_copy(u_hbm, u_ext.at[pl.ds(1, rows)], local_sem)
    own.start()
    pl.semaphore_wait(barrier, 4)

    def remote(src, dst, send, recv, target):
        return pltpu.make_async_remote_copy(
            src_ref=src, dst_ref=dst, send_sem=send, recv_sem=recv,
            device_id=target, device_id_type=pl.DeviceIdType.MESH)

    towards = (lower, upper)

    def row_copy(side, r):
        return remote(u_hbm.at[r], v_ext.at[side, r + 1], main_send.at[side, r], main_recv.at[side, r], towards[side])

    def halo_up(side):
        return remote(v_ext.at[side, rows], v_ext.at[side, 0], halo_send.at[4 + side], halo_recv.at[4 + side], above)

    def halo_down(side):
        return remote(v_ext.at[side, 1], v_ext.at[side, rows + 1], halo_send.at[6 + side], halo_recv.at[6 + side], below)

    coef_copy = remote(ct_hbm, ct_in, halo_send.at[0], halo_recv.at[0], upper)
    last_copy = remote(u_hbm.at[rows - 1], u_ext.at[0], halo_send.at[1], halo_recv.at[1], above)
    first_copy = remote(u_hbm.at[0], u_ext.at[rows + 1], halo_send.at[2], halo_recv.at[2], below)
    kx_copy = remote(kx_hbm.at[:, pl.ds(rows - 8, 8), :], kx_in, halo_send.at[3], halo_recv.at[3], above)

    for side in range(sides):
        row_copy(side, rows - 1).start()
        row_copy(side, 0).start()
    coef_copy.start()
    last_copy.start()
    first_copy.start()
    kx_copy.start()
    for side in range(sides):
        @pl.loop(1, rows - 1)
        def _(r):
            row_copy(side, r).start()

    for side in range(sides):
        row_copy(side, rows - 1).wait_recv()
        halo_up(side).start()
        row_copy(side, 0).wait_recv()
        halo_down(side).start()
    own.wait()
    coef_copy.wait_recv()
    last_copy.wait_recv()
    first_copy.wait_recv()
    kx_copy.wait_recv()
    for side in range(sides):
        halo_up(side).wait_recv()
        halo_down(side).wait_recv()

    @pl.when(space == n_space - 1)
    def _():
        u_ext[rows + 1] = jnp.zeros((mb, ny), jnp.bfloat16)
        for side in range(sides):
            v_ext[side, rows + 1] = jnp.zeros((mb, ny), jnp.bfloat16)

    coef = a_ref[...] + ct_in[...]
    pair = jnp.concatenate([coef, -coef], axis=1)

    def stack(e, cols):
        u = u_ext[e, :, cols]
        vs = [v_ext[side, e, :, cols] for side in range(sides)]
        return [u, u, vs[0], vs[-1]]

    def weighted(diff, weight_of):
        total = None
        for k in range(terms):
            part = weight_of(k) * diff[k * mb:(k + 1) * mb]
            total = part if total is None else total + part
        return total

    def flux_x(e, cols, weight_of):
        diff = jnp.dot(pair, jnp.concatenate(stack(e + 1, cols) + stack(e, cols), axis=0),
                       preferred_element_type=jnp.float32)
        return weighted(diff, weight_of)

    blocks = [pl.ds(c, LANES) for c in range(0, ny, LANES)]
    keep = jnp.where(space == 0, 0.0, 1.0).astype(jnp.float32)
    for cols in blocks:
        fx_prev[:, cols] = flux_x(0, cols, lambda k: kx_in[k, 7:8, cols]) * keep

    def shifted(x):
        lane = lax.broadcasted_iota(jnp.int32, x.shape, 1)
        moved = pltpu.roll(x.astype(jnp.float32), ny - 1, axis=1)
        return jnp.where(lane == ny - 1, 0.0, moved).astype(jnp.bfloat16)

    def row(r):
        e = r + 1
        sh[0] = shifted(u_ext[e])
        for side in range(sides):
            sh[1 + side] = shifted(v_ext[side, e])
        for cols in blocks:
            fx = flux_x(e, cols, lambda k: kx_ref[k, pl.ds(r, 1), cols])
            ahead = [sh[0, :, cols]] * 2 + [sh[1, :, cols], sh[sides, :, cols]]
            diff = jnp.dot(pair, jnp.concatenate(ahead + stack(e, cols), axis=0),
                           preferred_element_type=jnp.float32)
            fy = weighted(diff, lambda k: ky_ref[k, pl.ds(r, 1), cols])
            out_ref[r, :, cols] = fx_prev[:, cols] - fx - fy
            fx_prev[:, cols] = fx
            fy_row[:, cols] = fy
        fy = fy_row[...]
        lane = lax.broadcasted_iota(jnp.int32, fy.shape, 1)
        out_ref[r] += jnp.where(lane == 0, 0.0, pltpu.roll(fy, 1, axis=1))

    @pl.loop(0, rows - 3)
    def _(r):
        for side in range(sides):
            row_copy(side, r + 1).wait_recv()
        row(r)

    for side in range(sides):
        row_copy(side, rows - 2).wait_recv()

    @pl.loop(rows - 3, rows)
    def _(r):
        row(r)

    for side in range(sides):
        @pl.loop(0, rows)
        def _(r):
            row_copy(side, r).wait_send()
        halo_up(side).wait_send()
        halo_down(side).wait_send()
    for copy in (coef_copy, last_copy, first_copy, kx_copy):
        copy.wait_send()


def shards(n_mode, n_space, field, kappa_x, kappa_y, coupling, pattern):
    mb, rows, ny = field.shape
    terms = kappa_x.shape[0]
    sides = 1 if n_mode == 2 else 2
    coef = jnp.where(pattern > 0, coupling, jnp.zeros(coupling.shape, jnp.bfloat16))
    half = coef[0] * 0.5
    tall = lambda x: x.reshape(terms * mb, mb)
    flip = lambda x: tall(jnp.swapaxes(x, 1, 2))
    own = jnp.concatenate(
        [tall(half), flip(half), tall(coef[1]), jnp.zeros((terms * mb, mb), jnp.bfloat16)], axis=1)
    sent = jnp.concatenate(
        [jnp.zeros((terms * mb, 3 * mb), jnp.bfloat16), flip(coef[1])], axis=1)
    vmem = pl.BlockSpec(memory_space=pltpu.VMEM)
    hbm = pl.BlockSpec(memory_space=pl.ANY)
    out = pl.pallas_call(
        functools.partial(kernel, n_mode, n_space),
        out_shape=jax.ShapeDtypeStruct((rows, mb, ny), jnp.float32),
        in_specs=[hbm, vmem, vmem, vmem, hbm, hbm],
        out_specs=vmem,
        scratch_shapes=[
            pltpu.VMEM((rows + 2, mb, ny), jnp.bfloat16),
            pltpu.VMEM((sides, rows + 2, mb, ny), jnp.bfloat16),
            pltpu.VMEM((terms * mb, 4 * mb), jnp.bfloat16),
            pltpu.VMEM((terms, 8, ny), jnp.float32),
            pltpu.VMEM((mb, ny), jnp.float32),
            pltpu.VMEM((mb, ny), jnp.float32),
            pltpu.VMEM((1 + sides, mb, ny), jnp.bfloat16),
            pltpu.SemaphoreType.DMA,
            pltpu.SemaphoreType.DMA((sides, rows)),
            pltpu.SemaphoreType.DMA((sides, rows)),
            pltpu.SemaphoreType.DMA((8,)),
            pltpu.SemaphoreType.DMA((8,)),
        ],
        compiler_params=pltpu.CompilerParams(collective_id=0, has_side_effects=True),
    )(jnp.swapaxes(field, 0, 1), kappa_x, kappa_y, own, sent, kappa_x)
    return jnp.swapaxes(out, 0, 1)


def solution(mesh):
    placed = (
        P("mode", "space", None),
        P(None, "space", None),
        P(None, "space", None),
        P("mode", None, None, None),
        P("mode", None, None, None),
    )
    return jax.shard_map(
        functools.partial(shards, mesh.shape["mode"], mesh.shape["space"]),
        mesh=mesh, in_specs=placed, out_specs=P("mode", "space", None), check_vma=False)
```

```python
import functools

import jax
import jax.numpy as jnp
from jax import lax
from jax.experimental import pallas as pl
from jax.experimental.pallas import tpu as pltpu
from jax.sharding import PartitionSpec as P

LANES = 256


def kernel(n_mode, n_space, u_hbm, kx_hbm, ky_hbm, coup_hbm, pat_hbm, out_ref,
           u_ext, v_ext, kx_ref, ky_ref, coup, pat, coup_in, pat_in, pair_ref,
           kx_in, fx_prev, fy_row, held, last_row, sh,
           local_sem, main_send, main_recv, halo_send, halo_recv):
    rows, mb, ny = u_hbm.shape
    terms = kx_hbm.shape[0]
    sides = v_ext.shape[0]
    mode = lax.axis_index("mode")
    space = lax.axis_index("space")
    above = {"space": lax.rem(space + 1, n_space)}
    below = {"space": lax.rem(space + n_space - 1, n_space)}
    upper = {"mode": lax.rem(mode + 1, n_mode)}
    lower = {"mode": lax.rem(mode + n_mode - 1, n_mode)}

    barrier = pltpu.get_barrier_semaphore()
    for target in (above, below, upper, lower):
        pl.semaphore_signal(barrier, inc=1, device_id=target, device_id_type=pl.DeviceIdType.MESH)
    pl.semaphore_wait(barrier, 4)

    def remote(src, dst, send, recv, target):
        return pltpu.make_async_remote_copy(
            src_ref=src, dst_ref=dst, send_sem=send, recv_sem=recv,
            device_id=target, device_id_type=pl.DeviceIdType.MESH)

    towards = (lower, upper)

    def row_copy(side, r):
        return remote(u_hbm.at[r], v_ext.at[side, r + 1], main_send.at[side, r], main_recv.at[side, r], towards[side])

    def halo_up(side):
        return remote(v_ext.at[side, rows], v_ext.at[side, 0], halo_send.at[4 + side], halo_recv.at[4 + side], above)

    def halo_down(side):
        return remote(v_ext.at[side, 1], v_ext.at[side, rows + 1], halo_send.at[6 + side], halo_recv.at[6 + side], below)

    coup_copy = remote(coup_hbm.at[1], coup_in, halo_send.at[0], halo_recv.at[0], upper)
    pat_copy = remote(pat_hbm.at[1], pat_in, halo_send.at[8], halo_recv.at[8], upper)
    last_copy = remote(u_hbm.at[rows - 1], u_ext.at[0], halo_send.at[1], halo_recv.at[1], above)
    first_copy = remote(u_hbm.at[0], u_ext.at[rows + 1], halo_send.at[2], halo_recv.at[2], below)
    kx_copy = remote(kx_hbm.at[:, pl.ds(rows - 8, 8), :], kx_in, halo_send.at[3], halo_recv.at[3], above)

    for side in range(sides):
        row_copy(side, rows - 1).start()
        row_copy(side, 0).start()
    coup_copy.start()
    pat_copy.start()
    last_copy.start()
    first_copy.start()
    kx_copy.start()
    for side in range(sides):
        @pl.loop(1, rows - 1)
        def _(r):
            row_copy(side, r).start()

    locals_ = [
        pltpu.make_async_copy(src, dst, local_sem.at[i])
        for i, (src, dst) in enumerate([
            (coup_hbm, coup), (pat_hbm, pat), (u_hbm, u_ext.at[pl.ds(1, rows)]),
            (kx_hbm, kx_ref), (ky_hbm, ky_ref)])]
    for copy in locals_:
        copy.start()

    for side in range(sides):
        row_copy(side, rows - 1).wait_recv()
        halo_up(side).start()
        row_copy(side, 0).wait_recv()
        halo_down(side).start()
    coup_copy.wait_recv()
    pat_copy.wait_recv()
    for copy in locals_:
        copy.wait()

    def masked(values, mask):
        return jnp.where(mask > 0, values.astype(jnp.float32), 0.0)

    def placed(block, slot, flip):
        shape = (mb, 4 * mb)
        spot = lax.broadcasted_iota(jnp.int32, shape, 0) + slot * mb
        place = jnp.where(lax.broadcasted_iota(jnp.int32, shape, 1) == spot, 1.0, 0.0).astype(jnp.bfloat16)
        return lax.dot_general(block.astype(jnp.bfloat16), place, (((0 if flip else 1,), (0,)), ((), ())),
                               preferred_element_type=jnp.float32)

    @pl.loop(0, terms)
    def _(k):
        half = masked(coup[0, k], pat[0, k]) * 0.5
        coef = (placed(half, 0, False) + placed(half, 1, True)
                + placed(masked(coup[1, k], pat[1, k]), 2, False)
                + placed(masked(coup_in[k], pat_in[k]), 3, True)).astype(jnp.bfloat16)
        at = pl.ds(pl.multiple_of(k * mb, mb), mb)
        pair_ref[at, :4 * mb] = coef
        pair_ref[at, 4 * mb:] = -coef

    last_copy.wait_recv()
    first_copy.wait_recv()
    kx_copy.wait_recv()
    for side in range(sides):
        halo_up(side).wait_recv()
        halo_down(side).wait_recv()

    @pl.when(space == n_space - 1)
    def _():
        u_ext[rows + 1] = jnp.zeros((mb, ny), jnp.bfloat16)
        for side in range(sides):
            v_ext[side, rows + 1] = jnp.zeros((mb, ny), jnp.bfloat16)

    pair = pair_ref[...]

    def stack(e, cols):
        u = u_ext[e, :, cols]
        vs = [v_ext[side, e, :, cols] for side in range(sides)]
        return [u, u, vs[0], vs[-1]]

    def weighted(diff, weight_of):
        total = None
        for k in range(terms):
            part = weight_of(k) * diff[k * mb:(k + 1) * mb]
            total = part if total is None else total + part
        return total

    def flux_x(e, cols, weight_of):
        diff = jnp.dot(pair, jnp.concatenate(stack(e + 1, cols) + stack(e, cols), axis=0),
                       preferred_element_type=jnp.float32)
        return weighted(diff, weight_of)

    blocks = [pl.ds(c, LANES) for c in range(0, ny, LANES)]
    keep = jnp.where(space == 0, 0.0, 1.0).astype(jnp.float32)
    for cols in blocks:
        fx_prev[:, cols] = flux_x(0, cols, lambda k: kx_in[k, 7:8, cols]) * keep

    def shifted(x):
        lane = lax.broadcasted_iota(jnp.int32, x.shape, 1)
        moved = pltpu.roll(x.astype(jnp.float32), ny - 1, axis=1)
        return jnp.where(lane == ny - 1, 0.0, moved).astype(jnp.bfloat16)

    def kx_row(r, cols):
        return lambda k: kx_ref[k, pl.ds(r, 1), cols]

    def flux_y_part(r):
        e = r + 1
        sh[0] = shifted(u_ext[e])
        for side in range(sides):
            sh[1 + side] = shifted(v_ext[side, e])
        for cols in blocks:
            ahead = [sh[0, :, cols]] * 2 + [sh[1, :, cols], sh[sides, :, cols]]
            diff = jnp.dot(pair, jnp.concatenate(ahead + stack(e, cols), axis=0),
                           preferred_element_type=jnp.float32)
            fy_row[:, cols] = weighted(diff, lambda k: ky_ref[k, pl.ds(r, 1), cols])
        fy = fy_row[...]
        lane = lax.broadcasted_iota(jnp.int32, fy.shape, 1)
        return jnp.where(lane == 0, 0.0, pltpu.roll(fy, 1, axis=1)) - fy

    def put(r, cols, value):
        for at in range(0, LANES, 128):
            tile = (cols.start + at) // 128
            start = (r // 8) * 8 * (ny // 128) + tile * 8 + r % 8
            out_ref[pl.ds(start, mb, stride=rows * (ny // 128)), :] = value[:, at:at + 128]

    def flux_x_step(r):
        for cols in blocks:
            fx = flux_x(r + 1, cols, kx_row(r, cols))
            put(r, cols, fx_prev[:, cols] - fx + held[:, cols])
            fx_prev[:, cols] = fx

    final = rows - 1
    last_row[...] = flux_y_part(final)
    for cols in blocks:
        last_row[:, cols] = last_row[:, cols] - flux_x(rows, cols, kx_row(final, cols))

    @pl.loop(0, rows - 3)
    def _(r):
        held[...] = flux_y_part(r)
        for side in range(sides):
            row_copy(side, r + 1).wait_recv()
        flux_x_step(r)

    held[...] = flux_y_part(rows - 3)
    for side in range(sides):
        row_copy(side, rows - 2).wait_recv()
    flux_x_step(rows - 3)
    held[...] = flux_y_part(rows - 2)
    flux_x_step(rows - 2)
    for cols in blocks:
        put(final, cols, last_row[:, cols] + fx_prev[:, cols])

    for side in range(sides):
        @pl.loop(0, rows)
        def _(r):
            row_copy(side, r).wait_send()
        halo_up(side).wait_send()
        halo_down(side).wait_send()
    for copy in (coup_copy, pat_copy, last_copy, first_copy, kx_copy):
        copy.wait_send()


def shards(n_mode, n_space, field, kappa_x, kappa_y, coupling, pattern):
    mb, rows, ny = field.shape
    terms = kappa_x.shape[0]
    sides = 1 if n_mode == 2 else 2
    vmem = pl.BlockSpec(memory_space=pltpu.VMEM)
    hbm = pl.BlockSpec(memory_space=pl.ANY)
    out = pl.pallas_call(
        functools.partial(kernel, n_mode, n_space),
        out_shape=jax.ShapeDtypeStruct((mb * rows * ny // 128, 128), jnp.float32),
        in_specs=[hbm] * 5,
        out_specs=vmem,
        scratch_shapes=[
            pltpu.VMEM((rows + 2, mb, ny), jnp.bfloat16),
            pltpu.VMEM((sides, rows + 2, mb, ny), jnp.bfloat16),
            pltpu.VMEM(kappa_x.shape, jnp.float32),
            pltpu.VMEM(kappa_y.shape, jnp.float32),
            pltpu.VMEM(coupling.shape, jnp.bfloat16),
            pltpu.VMEM(pattern.shape, jnp.int32),
            pltpu.VMEM(coupling.shape[1:], jnp.bfloat16),
            pltpu.VMEM(pattern.shape[1:], jnp.int32),
            pltpu.VMEM((terms * mb, 8 * mb), jnp.bfloat16),
            pltpu.VMEM((terms, 8, ny), jnp.float32),
            pltpu.VMEM((mb, ny), jnp.float32),
            pltpu.VMEM((mb, ny), jnp.float32),
            pltpu.VMEM((mb, ny), jnp.float32),
            pltpu.VMEM((mb, ny), jnp.float32),
            pltpu.VMEM((1 + sides, mb, ny), jnp.bfloat16),
            pltpu.SemaphoreType.DMA((5,)),
            pltpu.SemaphoreType.DMA((sides, rows)),
            pltpu.SemaphoreType.DMA((sides, rows)),
            pltpu.SemaphoreType.DMA((9,)),
            pltpu.SemaphoreType.DMA((9,)),
        ],
        compiler_params=pltpu.CompilerParams(collective_id=0, has_side_effects=True, vmem_limit_bytes=24 * 2**20),
    )(jnp.swapaxes(field, 0, 1), kappa_x, kappa_y, coupling, pattern)
    tiles = out.reshape(mb, rows // 8, ny // 128, 8, 128)
    return jnp.swapaxes(tiles, 2, 3).reshape(mb, rows, ny)


def solution(mesh):
    placed = (
        P("mode", "space", None),
        P(None, "space", None),
        P(None, "space", None),
        P("mode", None, None, None),
        P("mode", None, None, None),
    )
    return jax.shard_map(
        functools.partial(shards, mesh.shape["mode"], mesh.shape["space"]),
        mesh=mesh, in_specs=placed, out_specs=P("mode", "space", None), check_vma=False)
```

```python
import functools

import jax
import jax.numpy as jnp
from jax import lax
from jax.experimental import pallas as pl
from jax.experimental.pallas import tpu as pltpu
from jax.sharding import PartitionSpec as P

LANES = 256


def kernel(n_mode, n_space, field_hbm, kx_hbm, ky_hbm, coup_hbm, pat_hbm, out_ref,
           raw, tall, u_ext, v_ext, kx_ref, ky_ref, coup, pat, packed, packed_in, pair_ref,
           kx_in, fx_prev, fy_row, held, last_row, sh,
           local_sem, main_send, main_recv, halo_send, halo_recv):
    mb, rows, ny = field_hbm.shape
    group = 128 // mb
    terms = kx_hbm.shape[0]
    sides = v_ext.shape[0]
    mode = lax.axis_index("mode")
    space = lax.axis_index("space")
    above = {"space": lax.rem(space + 1, n_space)}
    below = {"space": lax.rem(space + n_space - 1, n_space)}
    upper = {"mode": lax.rem(mode + 1, n_mode)}
    lower = {"mode": lax.rem(mode + n_mode - 1, n_mode)}

    barrier = pltpu.get_barrier_semaphore()
    for target in (above, below, upper, lower):
        pl.semaphore_signal(barrier, inc=1, device_id=target, device_id_type=pl.DeviceIdType.MESH)
    locals_ = [
        pltpu.make_async_copy(src, dst, local_sem.at[i])
        for i, (src, dst) in enumerate([
            (field_hbm, raw), (coup_hbm, coup), (pat_hbm, pat), (kx_hbm, kx_ref), (ky_hbm, ky_ref)])]
    for copy in locals_:
        copy.start()

    def masked(slot, k):
        return jnp.where(pat[slot, k] > 0, coup[slot, k].astype(jnp.float32), 0.0)

    def placed(block, shape, offset, flip=False):
        spot = lax.broadcasted_iota(jnp.int32, shape, 0) + offset
        place = jnp.where(lax.broadcasted_iota(jnp.int32, shape, 1) == spot, 1.0, 0.0).astype(jnp.bfloat16)
        return lax.dot_general(block.astype(jnp.bfloat16), place, (((0 if flip else 1,), (0,)), ((), ())),
                               preferred_element_type=jnp.float32)

    locals_[0].wait()
    for c in range(0, ny, 128):
        tall[...] = raw[:, :, c:c + 128].astype(jnp.float32).reshape(mb * rows, 128)
        for r in range(rows):
            u_ext[r + 1, :, c:c + 128] = tall[pl.ds(r, mb, stride=rows), :].astype(jnp.bfloat16)

    locals_[1].wait()
    locals_[2].wait()
    for q in range(terms // group):
        beside = None
        for p in range(group):
            part = placed(masked(1, q * group + p), (mb, 128), p * mb, flip=True)
            beside = part if beside is None else beside + part
        packed[q * mb:(q + 1) * mb] = beside.astype(jnp.bfloat16)

    pl.semaphore_wait(barrier, 4)

    def remote(src, dst, send, recv, target):
        return pltpu.make_async_remote_copy(
            src_ref=src, dst_ref=dst, send_sem=send, recv_sem=recv,
            device_id=target, device_id_type=pl.DeviceIdType.MESH)

    towards = (lower, upper)

    def row_copy(side, r):
        return remote(u_ext.at[r + 1], v_ext.at[side, r + 1], main_send.at[side, r], main_recv.at[side, r], towards[side])

    def halo_up(side):
        return remote(v_ext.at[side, rows], v_ext.at[side, 0], halo_send.at[4 + side], halo_recv.at[4 + side], above)

    def halo_down(side):
        return remote(v_ext.at[side, 1], v_ext.at[side, rows + 1], halo_send.at[6 + side], halo_recv.at[6 + side], below)

    coup_copy = remote(packed, packed_in, halo_send.at[0], halo_recv.at[0], upper)
    last_copy = remote(u_ext.at[rows], u_ext.at[0], halo_send.at[1], halo_recv.at[1], above)
    first_copy = remote(u_ext.at[1], u_ext.at[rows + 1], halo_send.at[2], halo_recv.at[2], below)
    kx_copy = remote(kx_hbm.at[:, pl.ds(rows - 8, 8), :], kx_in, halo_send.at[3], halo_recv.at[3], above)

    for side in range(sides):
        row_copy(side, rows - 1).start()
        row_copy(side, 0).start()
    coup_copy.start()
    last_copy.start()
    first_copy.start()
    kx_copy.start()
    for side in range(sides):
        @pl.loop(1, rows - 1)
        def _(r):
            row_copy(side, r).start()

    for side in range(sides):
        row_copy(side, rows - 1).wait_recv()
        halo_up(side).start()
        row_copy(side, 0).wait_recv()
        halo_down(side).start()
    coup_copy.wait_recv()
    for copy in locals_[3:]:
        copy.wait()

    for k in range(terms):
        q, p = divmod(k, group)
        half = masked(0, k) * 0.5
        shape = (mb, 4 * mb)
        coef = (placed(half, shape, 0) + placed(half, shape, mb, flip=True) + placed(masked(1, k), shape, 2 * mb)
                + placed(packed_in[q * mb:(q + 1) * mb, p * mb:(p + 1) * mb], shape, 3 * mb)).astype(jnp.bfloat16)
        pair_ref[k * mb:(k + 1) * mb, :4 * mb] = coef
        pair_ref[k * mb:(k + 1) * mb, 4 * mb:] = -coef

    last_copy.wait_recv()
    first_copy.wait_recv()
    kx_copy.wait_recv()
    for side in range(sides):
        halo_up(side).wait_recv()
        halo_down(side).wait_recv()

    @pl.when(space == n_space - 1)
    def _():
        u_ext[rows + 1] = jnp.zeros((mb, ny), jnp.bfloat16)
        for side in range(sides):
            v_ext[side, rows + 1] = jnp.zeros((mb, ny), jnp.bfloat16)

    pair = pair_ref[...]

    def stack(e, cols):
        u = u_ext[e, :, cols]
        vs = [v_ext[side, e, :, cols] for side in range(sides)]
        return [u, u, vs[0], vs[-1]]

    def weighted(diff, weight_of):
        total = None
        for k in range(terms):
            part = weight_of(k) * diff[k * mb:(k + 1) * mb]
            total = part if total is None else total + part
        return total

    def flux_x(e, cols, weight_of):
        diff = jnp.dot(pair, jnp.concatenate(stack(e + 1, cols) + stack(e, cols), axis=0),
                       preferred_element_type=jnp.float32)
        return weighted(diff, weight_of)

    blocks = [pl.ds(c, LANES) for c in range(0, ny, LANES)]
    keep = jnp.where(space == 0, 0.0, 1.0).astype(jnp.float32)
    for cols in blocks:
        fx_prev[:, cols] = flux_x(0, cols, lambda k: kx_in[k, 7:8, cols]) * keep

    def shifted(x):
        lane = lax.broadcasted_iota(jnp.int32, x.shape, 1)
        moved = pltpu.roll(x.astype(jnp.float32), ny - 1, axis=1)
        return jnp.where(lane == ny - 1, 0.0, moved).astype(jnp.bfloat16)

    def kx_row(r, cols):
        return lambda k: kx_ref[k, pl.ds(r, 1), cols]

    def flux_y_part(r):
        e = r + 1
        sh[0] = shifted(u_ext[e])
        for side in range(sides):
            sh[1 + side] = shifted(v_ext[side, e])
        for cols in blocks:
            ahead = [sh[0, :, cols]] * 2 + [sh[1, :, cols], sh[sides, :, cols]]
            diff = jnp.dot(pair, jnp.concatenate(ahead + stack(e, cols), axis=0),
                           preferred_element_type=jnp.float32)
            fy_row[:, cols] = weighted(diff, lambda k: ky_ref[k, pl.ds(r, 1), cols])
        fy = fy_row[...]
        lane = lax.broadcasted_iota(jnp.int32, fy.shape, 1)
        return jnp.where(lane == 0, 0.0, pltpu.roll(fy, 1, axis=1)) - fy

    def put(r, cols, value):
        for at in range(0, LANES, 128):
            tile = (cols.start + at) // 128
            start = (r // 8) * 8 * (ny // 128) + tile * 8 + r % 8
            out_ref[pl.ds(start, mb, stride=rows * (ny // 128)), :] = value[:, at:at + 128]

    def flux_x_step(r):
        for cols in blocks:
            fx = flux_x(r + 1, cols, kx_row(r, cols))
            put(r, cols, fx_prev[:, cols] - fx + held[:, cols])
            fx_prev[:, cols] = fx

    final = rows - 1
    last_row[...] = flux_y_part(final)
    for cols in blocks:
        last_row[:, cols] = last_row[:, cols] - flux_x(rows, cols, kx_row(final, cols))

    @pl.loop(0, rows - 3)
    def _(r):
        held[...] = flux_y_part(r)
        for side in range(sides):
            row_copy(side, r + 1).wait_recv()
        flux_x_step(r)

    held[...] = flux_y_part(rows - 3)
    for side in range(sides):
        row_copy(side, rows - 2).wait_recv()
    flux_x_step(rows - 3)
    held[...] = flux_y_part(rows - 2)
    flux_x_step(rows - 2)
    for cols in blocks:
        put(final, cols, last_row[:, cols] + fx_prev[:, cols])

    for side in range(sides):
        @pl.loop(0, rows)
        def _(r):
            row_copy(side, r).wait_send()
        halo_up(side).wait_send()
        halo_down(side).wait_send()
    for copy in (coup_copy, last_copy, first_copy, kx_copy):
        copy.wait_send()


def shards(n_mode, n_space, field, kappa_x, kappa_y, coupling, pattern):
    mb, rows, ny = field.shape
    terms = kappa_x.shape[0]
    sides = 1 if n_mode == 2 else 2
    vmem = pl.BlockSpec(memory_space=pltpu.VMEM)
    hbm = pl.BlockSpec(memory_space=pltpu.HBM)
    out = pl.pallas_call(
        functools.partial(kernel, n_mode, n_space),
        out_shape=jax.ShapeDtypeStruct((mb * rows * ny // 128, 128), jnp.float32),
        in_specs=[hbm] * 5,
        out_specs=vmem,
        scratch_shapes=[
            pltpu.VMEM(field.shape, jnp.bfloat16),
            pltpu.VMEM((mb * rows, 128), jnp.float32),
            pltpu.VMEM((rows + 2, mb, ny), jnp.bfloat16),
            pltpu.VMEM((sides, rows + 2, mb, ny), jnp.bfloat16),
            pltpu.VMEM(kappa_x.shape, jnp.float32),
            pltpu.VMEM(kappa_y.shape, jnp.float32),
            pltpu.VMEM(coupling.shape, jnp.bfloat16),
            pltpu.VMEM(pattern.shape, jnp.int32),
            pltpu.VMEM((terms * mb * mb // 128, 128), jnp.bfloat16),
            pltpu.VMEM((terms * mb * mb // 128, 128), jnp.bfloat16),
            pltpu.VMEM((terms * mb, 8 * mb), jnp.bfloat16),
            pltpu.VMEM((terms, 8, ny), jnp.float32),
            pltpu.VMEM((mb, ny), jnp.float32),
            pltpu.VMEM((mb, ny), jnp.float32),
            pltpu.VMEM((mb, ny), jnp.float32),
            pltpu.VMEM((mb, ny), jnp.float32),
            pltpu.VMEM((1 + sides, mb, ny), jnp.bfloat16),
            pltpu.SemaphoreType.DMA((5,)),
            pltpu.SemaphoreType.DMA((sides, rows)),
            pltpu.SemaphoreType.DMA((sides, rows)),
            pltpu.SemaphoreType.DMA((9,)),
            pltpu.SemaphoreType.DMA((9,)),
        ],
        compiler_params=pltpu.CompilerParams(collective_id=0, has_side_effects=True, vmem_limit_bytes=24 * 2**20),
    )(*[pltpu.with_memory_space_constraint(x, pltpu.HBM)
        for x in (field, kappa_x, kappa_y, coupling, pattern)])
    tiles = out.reshape(mb, rows // 8, ny // 128, 8, 128)
    return jnp.swapaxes(tiles, 2, 3).reshape(mb, rows, ny)


def solution(mesh):
    placed = (
        P("mode", "space", None),
        P(None, "space", None),
        P(None, "space", None),
        P("mode", None, None, None),
        P("mode", None, None, None),
    )
    return jax.shard_map(
        functools.partial(shards, mesh.shape["mode"], mesh.shape["space"]),
        mesh=mesh, in_specs=placed, out_specs=P("mode", "space", None), check_vma=False)
```

```python
import functools

import jax
import jax.numpy as jnp
from jax import lax
from jax.experimental import pallas as pl
from jax.experimental.pallas import tpu as pltpu
from jax.sharding import PartitionSpec as P

LANES = 256
HEAD = 128


def kernel(n_mode, n_space, field_hbm, kx_hbm, ky_hbm, coup_hbm, pat_hbm, out_ref,
           raw, tall, v_raw, u_ext, v_ext, kx_ref, ky_ref, coup, pat, packed, packed_in, pair_ref,
           kx_in, fx_prev, fy_row, held, last_row, sh,
           local_sem, head_send, head_recv, main_send, main_recv, halo_send, halo_recv):
    mb, rows, ny = field_hbm.shape
    group = 128 // mb
    terms = kx_hbm.shape[0]
    sides = v_ext.shape[0]
    mode = lax.axis_index("mode")
    space = lax.axis_index("space")
    above = {"space": lax.rem(space + 1, n_space)}
    below = {"space": lax.rem(space + n_space - 1, n_space)}
    upper = {"mode": lax.rem(mode + 1, n_mode)}
    lower = {"mode": lax.rem(mode + n_mode - 1, n_mode)}

    barrier = pltpu.get_barrier_semaphore()
    for target in (above, below, upper, lower):
        pl.semaphore_signal(barrier, inc=1, device_id=target, device_id_type=pl.DeviceIdType.MESH)
    locals_ = [
        pltpu.make_async_copy(src, dst, local_sem.at[i])
        for i, (src, dst) in enumerate([
            (field_hbm, raw), (coup_hbm, coup), (pat_hbm, pat), (kx_hbm, kx_ref), (ky_hbm, ky_ref)])]
    for copy in locals_:
        copy.start()

    pl.semaphore_wait(barrier, 4)

    def remote(src, dst, send, recv, target):
        return pltpu.make_async_remote_copy(
            src_ref=src, dst_ref=dst, send_sem=send, recv_sem=recv,
            device_id=target, device_id_type=pl.DeviceIdType.MESH)

    towards = (lower, upper)

    def row_copy(side, r):
        rest = pl.ds(HEAD, ny - HEAD)
        return remote(u_ext.at[r + 1, :, rest], v_ext.at[side, r + 1, :, rest], main_send.at[side, r], main_recv.at[side, r], towards[side])

    def head_copy(side):
        return remote(field_hbm.at[:, :, pl.ds(0, HEAD)], v_raw.at[side], head_send.at[side], head_recv.at[side], towards[side])

    def halo_up(side):
        return remote(v_ext.at[side, rows], v_ext.at[side, 0], halo_send.at[4 + side], halo_recv.at[4 + side], above)

    def halo_down(side):
        return remote(v_ext.at[side, 1], v_ext.at[side, rows + 1], halo_send.at[6 + side], halo_recv.at[6 + side], below)

    kx_copy = remote(kx_hbm.at[:, pl.ds(rows - 8, 8), :], kx_in, halo_send.at[3], halo_recv.at[3], above)
    for side in range(sides):
        head_copy(side).start()
    kx_copy.start()

    def masked(slot, k):
        return jnp.where(pat[slot, k] > 0, coup[slot, k].astype(jnp.float32), 0.0)

    def placed(block, shape, offset, flip=False):
        spot = lax.broadcasted_iota(jnp.int32, shape, 0) + offset
        place = jnp.where(lax.broadcasted_iota(jnp.int32, shape, 1) == spot, 1.0, 0.0).astype(jnp.bfloat16)
        return lax.dot_general(block.astype(jnp.bfloat16), place, (((0 if flip else 1,), (0,)), ((), ())),
                               preferred_element_type=jnp.float32)

    locals_[1].wait()
    locals_[2].wait()
    for q in range(terms // group):
        beside = None
        for p in range(group):
            part = placed(masked(1, q * group + p), (mb, 128), p * mb, flip=True)
            beside = part if beside is None else beside + part
        packed[q * mb:(q + 1) * mb] = beside.astype(jnp.bfloat16)

    def by_rows(source, source_at, target, at):
        tall[...] = source[:, :, source_at:source_at + 128].astype(jnp.float32).reshape(mb * rows, 128)
        for r in range(rows):
            target[r + 1, :, at:at + 128] = tall[pl.ds(r, mb, stride=rows), :].astype(jnp.bfloat16)

    locals_[0].wait()
    for c in range(0, ny, 128):
        by_rows(raw, c, u_ext, c)

    coup_copy = remote(packed, packed_in, halo_send.at[0], halo_recv.at[0], upper)
    last_copy = remote(u_ext.at[rows], u_ext.at[0], halo_send.at[1], halo_recv.at[1], above)
    first_copy = remote(u_ext.at[1], u_ext.at[rows + 1], halo_send.at[2], halo_recv.at[2], below)

    for side in range(sides):
        row_copy(side, rows - 1).start()
        row_copy(side, 0).start()
    coup_copy.start()
    last_copy.start()
    first_copy.start()
    for side in range(sides):
        @pl.loop(1, rows - 1)
        def _(r):
            row_copy(side, r).start()

    for side in range(sides):
        head_copy(side).wait_recv()
        for c in range(0, HEAD, 128):
            by_rows(v_raw.at[side], c, v_ext.at[side], c)
    for side in range(sides):
        row_copy(side, rows - 1).wait_recv()
        halo_up(side).start()
        row_copy(side, 0).wait_recv()
        halo_down(side).start()
    coup_copy.wait_recv()
    for copy in locals_[3:]:
        copy.wait()

    for k in range(terms):
        q, p = divmod(k, group)
        half = masked(0, k) * 0.5
        shape = (mb, 4 * mb)
        coef = (placed(half, shape, 0) + placed(half, shape, mb, flip=True) + placed(masked(1, k), shape, 2 * mb)
                + placed(packed_in[q * mb:(q + 1) * mb, p * mb:(p + 1) * mb], shape, 3 * mb)).astype(jnp.bfloat16)
        pair_ref[k * mb:(k + 1) * mb, :4 * mb] = coef
        pair_ref[k * mb:(k + 1) * mb, 4 * mb:] = -coef

    last_copy.wait_recv()
    first_copy.wait_recv()
    kx_copy.wait_recv()
    for side in range(sides):
        halo_up(side).wait_recv()
        halo_down(side).wait_recv()

    @pl.when(space == n_space - 1)
    def _():
        u_ext[rows + 1] = jnp.zeros((mb, ny), jnp.bfloat16)
        for side in range(sides):
            v_ext[side, rows + 1] = jnp.zeros((mb, ny), jnp.bfloat16)

    pair = pair_ref[...]

    def stack(e, cols):
        u = u_ext[e, :, cols]
        vs = [v_ext[side, e, :, cols] for side in range(sides)]
        return [u, u, vs[0], vs[-1]]

    def weighted(diff, weight_of):
        total = None
        for k in range(terms):
            part = weight_of(k) * diff[k * mb:(k + 1) * mb]
            total = part if total is None else total + part
        return total

    def flux_x(e, cols, weight_of):
        diff = jnp.dot(pair, jnp.concatenate(stack(e + 1, cols) + stack(e, cols), axis=0),
                       preferred_element_type=jnp.float32)
        return weighted(diff, weight_of)

    blocks = [pl.ds(c, LANES) for c in range(0, ny, LANES)]
    keep = jnp.where(space == 0, 0.0, 1.0).astype(jnp.float32)
    for cols in blocks:
        fx_prev[:, cols] = flux_x(0, cols, lambda k: kx_in[k, 7:8, cols]) * keep

    def shifted(x):
        lane = lax.broadcasted_iota(jnp.int32, x.shape, 1)
        moved = pltpu.roll(x.astype(jnp.float32), ny - 1, axis=1)
        return jnp.where(lane == ny - 1, 0.0, moved).astype(jnp.bfloat16)

    def kx_row(r, cols):
        return lambda k: kx_ref[k, pl.ds(r, 1), cols]

    def flux_y_part(r):
        e = r + 1
        sh[0] = shifted(u_ext[e])
        for side in range(sides):
            sh[1 + side] = shifted(v_ext[side, e])
        for cols in blocks:
            ahead = [sh[0, :, cols]] * 2 + [sh[1, :, cols], sh[sides, :, cols]]
            diff = jnp.dot(pair, jnp.concatenate(ahead + stack(e, cols), axis=0),
                           preferred_element_type=jnp.float32)
            fy_row[:, cols] = weighted(diff, lambda k: ky_ref[k, pl.ds(r, 1), cols])
        fy = fy_row[...]
        lane = lax.broadcasted_iota(jnp.int32, fy.shape, 1)
        return jnp.where(lane == 0, 0.0, pltpu.roll(fy, 1, axis=1)) - fy

    def put(r, cols, value):
        for at in range(0, LANES, 128):
            tile = (cols.start + at) // 128
            start = (r // 8) * 8 * (ny // 128) + tile * 8 + r % 8
            out_ref[pl.ds(start, mb, stride=rows * (ny // 128)), :] = value[:, at:at + 128]

    def flux_x_step(r):
        for cols in blocks:
            fx = flux_x(r + 1, cols, kx_row(r, cols))
            put(r, cols, fx_prev[:, cols] - fx + held[:, cols])
            fx_prev[:, cols] = fx

    final = rows - 1
    last_row[...] = flux_y_part(final)
    for cols in blocks:
        last_row[:, cols] = last_row[:, cols] - flux_x(rows, cols, kx_row(final, cols))

    @pl.loop(0, rows - 3)
    def _(r):
        held[...] = flux_y_part(r)
        for side in range(sides):
            row_copy(side, r + 1).wait_recv()
        flux_x_step(r)

    held[...] = flux_y_part(rows - 3)
    for side in range(sides):
        row_copy(side, rows - 2).wait_recv()
    flux_x_step(rows - 3)
    held[...] = flux_y_part(rows - 2)
    flux_x_step(rows - 2)
    for cols in blocks:
        put(final, cols, last_row[:, cols] + fx_prev[:, cols])

    for side in range(sides):
        @pl.loop(0, rows)
        def _(r):
            row_copy(side, r).wait_send()
        head_copy(side).wait_send()
        halo_up(side).wait_send()
        halo_down(side).wait_send()
    for copy in (coup_copy, last_copy, first_copy, kx_copy):
        copy.wait_send()


def shards(n_mode, n_space, field, kappa_x, kappa_y, coupling, pattern):
    mb, rows, ny = field.shape
    terms = kappa_x.shape[0]
    sides = 1 if n_mode == 2 else 2
    vmem = pl.BlockSpec(memory_space=pltpu.VMEM)
    hbm = pl.BlockSpec(memory_space=pltpu.HBM)
    out = pl.pallas_call(
        functools.partial(kernel, n_mode, n_space),
        out_shape=jax.ShapeDtypeStruct((mb * rows * ny // 128, 128), jnp.float32),
        in_specs=[hbm] * 5,
        out_specs=vmem,
        scratch_shapes=[
            pltpu.VMEM(field.shape, jnp.bfloat16),
            pltpu.VMEM((mb * rows, 128), jnp.float32),
            pltpu.VMEM((sides, mb, rows, HEAD), jnp.bfloat16),
            pltpu.VMEM((rows + 2, mb, ny), jnp.bfloat16),
            pltpu.VMEM((sides, rows + 2, mb, ny), jnp.bfloat16),
            pltpu.VMEM(kappa_x.shape, jnp.float32),
            pltpu.VMEM(kappa_y.shape, jnp.float32),
            pltpu.VMEM(coupling.shape, jnp.bfloat16),
            pltpu.VMEM(pattern.shape, jnp.int32),
            pltpu.VMEM((terms * mb * mb // 128, 128), jnp.bfloat16),
            pltpu.VMEM((terms * mb * mb // 128, 128), jnp.bfloat16),
            pltpu.VMEM((terms * mb, 8 * mb), jnp.bfloat16),
            pltpu.VMEM((terms, 8, ny), jnp.float32),
            pltpu.VMEM((mb, ny), jnp.float32),
            pltpu.VMEM((mb, ny), jnp.float32),
            pltpu.VMEM((mb, ny), jnp.float32),
            pltpu.VMEM((mb, ny), jnp.float32),
            pltpu.VMEM((1 + sides, mb, ny), jnp.bfloat16),
            pltpu.SemaphoreType.DMA((5,)),
            pltpu.SemaphoreType.DMA((sides,)),
            pltpu.SemaphoreType.DMA((sides,)),
            pltpu.SemaphoreType.DMA((sides, rows)),
            pltpu.SemaphoreType.DMA((sides, rows)),
            pltpu.SemaphoreType.DMA((9,)),
            pltpu.SemaphoreType.DMA((9,)),
        ],
        compiler_params=pltpu.CompilerParams(collective_id=0, has_side_effects=True, vmem_limit_bytes=24 * 2**20),
    )(*[pltpu.with_memory_space_constraint(x, pltpu.HBM)
        for x in (field, kappa_x, kappa_y, coupling, pattern)])
    tiles = out.reshape(mb, rows // 8, ny // 128, 8, 128)
    return jnp.swapaxes(tiles, 2, 3).reshape(mb, rows, ny)


def solution(mesh):
    placed = (
        P("mode", "space", None),
        P(None, "space", None),
        P(None, "space", None),
        P("mode", None, None, None),
        P("mode", None, None, None),
    )
    return jax.shard_map(
        functools.partial(shards, mesh.shape["mode"], mesh.shape["space"]),
        mesh=mesh, in_specs=placed, out_specs=P("mode", "space", None), check_vma=False)
```

```python
import functools

import jax
import jax.numpy as jnp
from jax import lax
from jax.experimental import pallas as pl
from jax.experimental.pallas import tpu as pltpu
from jax.sharding import PartitionSpec as P

LANES = 256
HEAD = 128


def kernel(n_mode, n_space, field_hbm, kx_hbm, ky_hbm, coup_hbm, pat_hbm, out_ref,
           raw, tall, v_raw, u_ext, v_ext, kx_ref, ky_ref, coup, pat, packed, packed_in, pair_ref,
           kx_in, fx_prev, fy_row, held, last_row, sh,
           local_sem, head_send, head_recv, piece_send, piece_recv, main_send, main_recv, halo_send, halo_recv):
    mb, rows, ny = field_hbm.shape
    group = 128 // mb
    terms = kx_hbm.shape[0]
    sides = v_ext.shape[0]
    mode = lax.axis_index("mode")
    space = lax.axis_index("space")
    above = {"space": lax.rem(space + 1, n_space)}
    below = {"space": lax.rem(space + n_space - 1, n_space)}
    upper = {"mode": lax.rem(mode + 1, n_mode)}
    lower = {"mode": lax.rem(mode + n_mode - 1, n_mode)}

    barrier = pltpu.get_barrier_semaphore()
    for target in (above, below, upper, lower):
        pl.semaphore_signal(barrier, inc=1, device_id=target, device_id_type=pl.DeviceIdType.MESH)
    locals_ = [
        pltpu.make_async_copy(src, dst, local_sem.at[i])
        for i, (src, dst) in enumerate([
            (field_hbm, raw), (coup_hbm, coup), (pat_hbm, pat), (kx_hbm, kx_ref), (ky_hbm, ky_ref)])]
    for copy in locals_:
        copy.start()

    pl.semaphore_wait(barrier, 4)

    def remote(src, dst, send, recv, target):
        return pltpu.make_async_remote_copy(
            src_ref=src, dst_ref=dst, send_sem=send, recv_sem=recv,
            device_id=target, device_id_type=pl.DeviceIdType.MESH)

    towards = (lower, upper)

    def row_copy(side, r):
        rest = pl.ds(HEAD, ny - HEAD)
        return remote(u_ext.at[r + 1, :, rest], v_ext.at[side, r + 1, :, rest], main_send.at[side, r], main_recv.at[side, r], towards[side])

    order = list(reversed(range(ny // LANES)))

    def piece_copy(side, b):
        cols = pl.ds(max(b * LANES, HEAD), min(LANES, (b + 1) * LANES - HEAD))
        return remote(u_ext.at[rows - 1, :, cols], v_ext.at[side, rows - 1, :, cols], piece_send.at[side, b], piece_recv.at[side, b], towards[side])

    def head_copy(side):
        return remote(field_hbm.at[:, :, pl.ds(0, HEAD)], v_raw.at[side], head_send.at[side], head_recv.at[side], towards[side])

    def halo_up(side):
        return remote(v_ext.at[side, rows], v_ext.at[side, 0], halo_send.at[4 + side], halo_recv.at[4 + side], above)

    def halo_down(side):
        return remote(v_ext.at[side, 1], v_ext.at[side, rows + 1], halo_send.at[6 + side], halo_recv.at[6 + side], below)

    kx_copy = remote(kx_hbm.at[:, pl.ds(rows - 8, 8), :], kx_in, halo_send.at[3], halo_recv.at[3], above)
    for side in range(sides):
        head_copy(side).start()
    kx_copy.start()

    def masked(slot, k):
        return jnp.where(pat[slot, k] > 0, coup[slot, k].astype(jnp.float32), 0.0)

    def placed(block, shape, offset, flip=False):
        spot = lax.broadcasted_iota(jnp.int32, shape, 0) + offset
        place = jnp.where(lax.broadcasted_iota(jnp.int32, shape, 1) == spot, 1.0, 0.0).astype(jnp.bfloat16)
        return lax.dot_general(block.astype(jnp.bfloat16), place, (((0 if flip else 1,), (0,)), ((), ())),
                               preferred_element_type=jnp.float32)

    locals_[1].wait()
    locals_[2].wait()
    for q in range(terms // group):
        beside = None
        for p in range(group):
            part = placed(masked(1, q * group + p), (mb, 128), p * mb, flip=True)
            beside = part if beside is None else beside + part
        packed[q * mb:(q + 1) * mb] = beside.astype(jnp.bfloat16)

    def by_rows(source, source_at, target, at):
        tall[...] = source[:, :, source_at:source_at + 128].astype(jnp.float32).reshape(mb * rows, 128)
        for r in range(rows):
            target[r + 1, :, at:at + 128] = tall[pl.ds(r, mb, stride=rows), :].astype(jnp.bfloat16)

    locals_[0].wait()
    for c in range(0, ny, 128):
        by_rows(raw, c, u_ext, c)

    coup_copy = remote(packed, packed_in, halo_send.at[0], halo_recv.at[0], upper)
    last_copy = remote(u_ext.at[rows], u_ext.at[0], halo_send.at[1], halo_recv.at[1], above)
    first_copy = remote(u_ext.at[1], u_ext.at[rows + 1], halo_send.at[2], halo_recv.at[2], below)

    for side in range(sides):
        row_copy(side, rows - 1).start()
        row_copy(side, 0).start()
    coup_copy.start()
    last_copy.start()
    first_copy.start()
    for side in range(sides):
        @pl.loop(1, rows - 2)
        def _(r):
            row_copy(side, r).start()
        for b in order:
            piece_copy(side, b).start()

    for side in range(sides):
        head_copy(side).wait_recv()
        for c in range(0, HEAD, 128):
            by_rows(v_raw.at[side], c, v_ext.at[side], c)
    for side in range(sides):
        row_copy(side, rows - 1).wait_recv()
        halo_up(side).start()
        row_copy(side, 0).wait_recv()
        halo_down(side).start()
    coup_copy.wait_recv()
    for copy in locals_[3:]:
        copy.wait()

    for k in range(terms):
        q, p = divmod(k, group)
        half = masked(0, k) * 0.5
        shape = (mb, 4 * mb)
        coef = (placed(half, shape, 0) + placed(half, shape, mb, flip=True) + placed(masked(1, k), shape, 2 * mb)
                + placed(packed_in[q * mb:(q + 1) * mb, p * mb:(p + 1) * mb], shape, 3 * mb)).astype(jnp.bfloat16)
        pair_ref[k * mb:(k + 1) * mb, :4 * mb] = coef
        pair_ref[k * mb:(k + 1) * mb, 4 * mb:] = -coef

    last_copy.wait_recv()
    first_copy.wait_recv()
    kx_copy.wait_recv()
    for side in range(sides):
        halo_up(side).wait_recv()
        halo_down(side).wait_recv()

    @pl.when(space == n_space - 1)
    def _():
        u_ext[rows + 1] = jnp.zeros((mb, ny), jnp.bfloat16)
        for side in range(sides):
            v_ext[side, rows + 1] = jnp.zeros((mb, ny), jnp.bfloat16)

    pair = pair_ref[...]

    def stack(e, cols):
        u = u_ext[e, :, cols]
        vs = [v_ext[side, e, :, cols] for side in range(sides)]
        return [u, u, vs[0], vs[-1]]

    def weighted(diff, weight_of):
        total = None
        for k in range(terms):
            part = weight_of(k) * diff[k * mb:(k + 1) * mb]
            total = part if total is None else total + part
        return total

    def flux_x(e, cols, weight_of):
        diff = jnp.dot(pair, jnp.concatenate(stack(e + 1, cols) + stack(e, cols), axis=0),
                       preferred_element_type=jnp.float32)
        return weighted(diff, weight_of)

    blocks = [pl.ds(c, LANES) for c in range(0, ny, LANES)]
    keep = jnp.where(space == 0, 0.0, 1.0).astype(jnp.float32)
    for cols in blocks:
        fx_prev[:, cols] = flux_x(0, cols, lambda k: kx_in[k, 7:8, cols]) * keep

    def shifted(x):
        lane = lax.broadcasted_iota(jnp.int32, x.shape, 1)
        moved = pltpu.roll(x.astype(jnp.float32), ny - 1, axis=1)
        return jnp.where(lane == ny - 1, 0.0, moved).astype(jnp.bfloat16)

    def kx_row(r, cols):
        return lambda k: kx_ref[k, pl.ds(r, 1), cols]

    def block_flux_y(r, cols):
        ahead = [sh[0, :, cols]] * 2 + [sh[1, :, cols], sh[sides, :, cols]]
        diff = jnp.dot(pair, jnp.concatenate(ahead + stack(r + 1, cols), axis=0),
                       preferred_element_type=jnp.float32)
        return weighted(diff, lambda k: ky_ref[k, pl.ds(r, 1), cols])

    def flux_y_part(r):
        e = r + 1
        sh[0] = shifted(u_ext[e])
        for side in range(sides):
            sh[1 + side] = shifted(v_ext[side, e])
        for cols in blocks:
            fy_row[:, cols] = block_flux_y(r, cols)
        fy = fy_row[...]
        lane = lax.broadcasted_iota(jnp.int32, fy.shape, 1)
        return jnp.where(lane == 0, 0.0, pltpu.roll(fy, 1, axis=1)) - fy

    def put(r, cols, value):
        for at in range(0, LANES, 128):
            tile = (cols.start + at) // 128
            start = (r // 8) * 8 * (ny // 128) + tile * 8 + r % 8
            out_ref[pl.ds(start, mb, stride=rows * (ny // 128)), :] = value[:, at:at + 128]

    def flux_x_step(r):
        for cols in blocks:
            fx = flux_x(r + 1, cols, kx_row(r, cols))
            put(r, cols, fx_prev[:, cols] - fx + held[:, cols])
            fx_prev[:, cols] = fx

    final = rows - 1
    last_row[...] = flux_y_part(final)
    for cols in blocks:
        last_row[:, cols] = last_row[:, cols] - flux_x(rows, cols, kx_row(final, cols))

    @pl.loop(0, rows - 3)
    def _(r):
        held[...] = flux_y_part(r)
        for side in range(sides):
            row_copy(side, r + 1).wait_recv()
        flux_x_step(r)

    held[...] = flux_y_part(rows - 3)
    e = rows - 1
    sh[0] = shifted(u_ext[e])

    def finish(b):
        start = b * LANES - (0 if b == 0 else 128)
        fy = fy_row[:, start:(b + 1) * LANES]
        moved = pltpu.roll(fy, 1, axis=1)
        if b == 0:
            moved = jnp.where(lax.broadcasted_iota(jnp.int32, fy.shape, 1) == 0, 0.0, moved)
        value = (moved - fy)[:, fy.shape[1] - LANES:]
        put(rows - 2, blocks[b], held[:, blocks[b]] + value)

    for b in order:
        cols = blocks[b]
        last = b == order[0]
        for side in range(sides):
            piece_copy(side, b).wait_recv()
            window = v_ext[side, e, :, b * LANES:(b + 1) * LANES + (0 if last else 128)].astype(jnp.float32)
            moved = pltpu.roll(window, window.shape[1] - 1, axis=1)
            if last:
                moved = jnp.where(lax.broadcasted_iota(jnp.int32, window.shape, 1) == LANES - 1, 0.0, moved)
            sh[1 + side, :, cols] = moved[:, :LANES].astype(jnp.bfloat16)
        before = flux_x(rows - 2, cols, kx_row(rows - 3, cols))
        fx = flux_x(e, cols, kx_row(rows - 2, cols))
        fy_row[:, cols] = block_flux_y(rows - 2, cols)
        put(rows - 3, cols, fx_prev[:, cols] - before + held[:, cols])
        held[:, cols] = before - fx
        put(final, cols, last_row[:, cols] + fx)
        if not last:
            finish(b + 1)
    finish(0)

    for side in range(sides):
        @pl.loop(0, rows - 2)
        def _(r):
            row_copy(side, r).wait_send()
        row_copy(side, rows - 1).wait_send()
        for b in order:
            piece_copy(side, b).wait_send()
        head_copy(side).wait_send()
        halo_up(side).wait_send()
        halo_down(side).wait_send()
    for copy in (coup_copy, last_copy, first_copy, kx_copy):
        copy.wait_send()


def shards(n_mode, n_space, field, kappa_x, kappa_y, coupling, pattern):
    mb, rows, ny = field.shape
    terms = kappa_x.shape[0]
    sides = 1 if n_mode == 2 else 2
    vmem = pl.BlockSpec(memory_space=pltpu.VMEM)
    hbm = pl.BlockSpec(memory_space=pltpu.HBM)
    out = pl.pallas_call(
        functools.partial(kernel, n_mode, n_space),
        out_shape=jax.ShapeDtypeStruct((mb * rows * ny // 128, 128), jnp.float32),
        in_specs=[hbm] * 5,
        out_specs=vmem,
        scratch_shapes=[
            pltpu.VMEM(field.shape, jnp.bfloat16),
            pltpu.VMEM((mb * rows, 128), jnp.float32),
            pltpu.VMEM((sides, mb, rows, HEAD), jnp.bfloat16),
            pltpu.VMEM((rows + 2, mb, ny), jnp.bfloat16),
            pltpu.VMEM((sides, rows + 2, mb, ny), jnp.bfloat16),
            pltpu.VMEM(kappa_x.shape, jnp.float32),
            pltpu.VMEM(kappa_y.shape, jnp.float32),
            pltpu.VMEM(coupling.shape, jnp.bfloat16),
            pltpu.VMEM(pattern.shape, jnp.int32),
            pltpu.VMEM((terms * mb * mb // 128, 128), jnp.bfloat16),
            pltpu.VMEM((terms * mb * mb // 128, 128), jnp.bfloat16),
            pltpu.VMEM((terms * mb, 8 * mb), jnp.bfloat16),
            pltpu.VMEM((terms, 8, ny), jnp.float32),
            pltpu.VMEM((mb, ny), jnp.float32),
            pltpu.VMEM((mb, ny), jnp.float32),
            pltpu.VMEM((mb, ny), jnp.float32),
            pltpu.VMEM((mb, ny), jnp.float32),
            pltpu.VMEM((1 + sides, mb, ny), jnp.bfloat16),
            pltpu.SemaphoreType.DMA((5,)),
            pltpu.SemaphoreType.DMA((sides,)),
            pltpu.SemaphoreType.DMA((sides,)),
            pltpu.SemaphoreType.DMA((sides, ny // LANES)),
            pltpu.SemaphoreType.DMA((sides, ny // LANES)),
            pltpu.SemaphoreType.DMA((sides, rows)),
            pltpu.SemaphoreType.DMA((sides, rows)),
            pltpu.SemaphoreType.DMA((9,)),
            pltpu.SemaphoreType.DMA((9,)),
        ],
        compiler_params=pltpu.CompilerParams(collective_id=0, has_side_effects=True, vmem_limit_bytes=24 * 2**20),
    )(*[pltpu.with_memory_space_constraint(x, pltpu.HBM)
        for x in (field, kappa_x, kappa_y, coupling, pattern)])
    tiles = out.reshape(mb, rows // 8, ny // 128, 8, 128)
    return jnp.swapaxes(tiles, 2, 3).reshape(mb, rows, ny)


def solution(mesh):
    placed = (
        P("mode", "space", None),
        P(None, "space", None),
        P(None, "space", None),
        P("mode", None, None, None),
        P("mode", None, None, None),
    )
    return jax.shard_map(
        functools.partial(shards, mesh.shape["mode"], mesh.shape["space"]),
        mesh=mesh, in_specs=placed, out_specs=P("mode", "space", None), check_vma=False)
```

```python
import functools

import jax
import jax.numpy as jnp
from jax import lax
from jax.experimental import pallas as pl
from jax.experimental.pallas import tpu as pltpu
from jax.sharding import PartitionSpec as P

LANES = 256


def kernel(n_mode, n_space, field_hbm, kx_hbm, ky_hbm, coup_hbm, pat_hbm, out_ref,
           raw, tall, u_ext, v_ext, kx_ref, ky_ref, coup, pat, packed, packed_in, pair_ref,
           kx_in, fx_prev, fy_row, held, last_row, sh,
           local_sem, main_send, main_recv, halo_send, halo_recv):
    mb, rows, ny = field_hbm.shape
    group = 128 // mb
    terms = kx_hbm.shape[0]
    sides = v_ext.shape[0]
    mode = lax.axis_index("mode")
    space = lax.axis_index("space")
    above = {"space": lax.rem(space + 1, n_space)}
    below = {"space": lax.rem(space + n_space - 1, n_space)}
    upper = {"mode": lax.rem(mode + 1, n_mode)}
    lower = {"mode": lax.rem(mode + n_mode - 1, n_mode)}

    barrier = pltpu.get_barrier_semaphore()
    for target in (above, below, upper, lower):
        pl.semaphore_signal(barrier, inc=1, device_id=target, device_id_type=pl.DeviceIdType.MESH)
    locals_ = [
        pltpu.make_async_copy(src, dst, local_sem.at[i])
        for i, (src, dst) in enumerate([
            (field_hbm.at[:, pl.ds(0, 8), :], raw.at[:, pl.ds(0, 8), :]),
            (field_hbm.at[:, pl.ds(8, rows - 8), :], raw.at[:, pl.ds(8, rows - 8), :]),
            (coup_hbm, coup), (pat_hbm, pat), (kx_hbm, kx_ref), (ky_hbm, ky_ref)])]
    for copy in locals_:
        copy.start()

    def masked(slot, k):
        return jnp.where(pat[slot, k] > 0, coup[slot, k].astype(jnp.float32), 0.0)

    def placed(block, shape, offset, flip=False):
        spot = lax.broadcasted_iota(jnp.int32, shape, 0) + offset
        place = jnp.where(lax.broadcasted_iota(jnp.int32, shape, 1) == spot, 1.0, 0.0).astype(jnp.bfloat16)
        return lax.dot_general(block.astype(jnp.bfloat16), place, (((0 if flip else 1,), (0,)), ((), ())),
                               preferred_element_type=jnp.float32)

    def by_rows(first, count):
        for c in range(0, ny, 128):
            tall[:mb * count] = raw[:, first:first + count, c:c + 128].astype(jnp.float32).reshape(mb * count, 128)
            for r in range(count):
                u_ext[first + r + 1, :, c:c + 128] = tall[pl.ds(r, mb, stride=count), :].astype(jnp.bfloat16)

    locals_[0].wait()
    by_rows(0, 8)
    pl.semaphore_wait(barrier, 4)

    def remote(src, dst, send, recv, target):
        return pltpu.make_async_remote_copy(
            src_ref=src, dst_ref=dst, send_sem=send, recv_sem=recv,
            device_id=target, device_id_type=pl.DeviceIdType.MESH)

    towards = (lower, upper)

    def row_copy(side, r):
        return remote(u_ext.at[r + 1], v_ext.at[side, r + 1], main_send.at[side, r], main_recv.at[side, r], towards[side])

    def halo_up(side):
        return remote(v_ext.at[side, rows], v_ext.at[side, 0], halo_send.at[4 + side], halo_recv.at[4 + side], above)

    def halo_down(side):
        return remote(v_ext.at[side, 1], v_ext.at[side, rows + 1], halo_send.at[6 + side], halo_recv.at[6 + side], below)

    coup_copy = remote(packed, packed_in, halo_send.at[0], halo_recv.at[0], upper)
    last_copy = remote(u_ext.at[rows], u_ext.at[0], halo_send.at[1], halo_recv.at[1], above)
    first_copy = remote(u_ext.at[1], u_ext.at[rows + 1], halo_send.at[2], halo_recv.at[2], below)
    kx_copy = remote(kx_hbm.at[:, pl.ds(rows - 8, 8), :], kx_in, halo_send.at[3], halo_recv.at[3], above)

    for side in range(sides):
        row_copy(side, 0).start()
    first_copy.start()
    kx_copy.start()
    locals_[1].wait()
    by_rows(8, rows - 8)
    for side in range(sides):
        row_copy(side, rows - 1).start()
        row_copy(side, 1).start()
        row_copy(side, 2).start()
    last_copy.start()

    locals_[2].wait()
    locals_[3].wait()
    for q in range(terms // group):
        beside = None
        for p in range(group):
            part = placed(masked(1, q * group + p), (mb, 128), p * mb, flip=True)
            beside = part if beside is None else beside + part
        packed[q * mb:(q + 1) * mb] = beside.astype(jnp.bfloat16)

    coup_copy.start()
    for side in range(sides):
        @pl.loop(3, rows - 1)
        def _(r):
            row_copy(side, r).start()

    for side in range(sides):
        row_copy(side, 0).wait_recv()
        halo_down(side).start()
        row_copy(side, rows - 1).wait_recv()
        halo_up(side).start()
    coup_copy.wait_recv()
    for copy in locals_[4:]:
        copy.wait()

    for k in range(terms):
        q, p = divmod(k, group)
        half = masked(0, k) * 0.5
        shape = (mb, 4 * mb)
        coef = (placed(half, shape, 0) + placed(half, shape, mb, flip=True) + placed(masked(1, k), shape, 2 * mb)
                + placed(packed_in[q * mb:(q + 1) * mb, p * mb:(p + 1) * mb], shape, 3 * mb)).astype(jnp.bfloat16)
        pair_ref[k * mb:(k + 1) * mb, :4 * mb] = coef
        pair_ref[k * mb:(k + 1) * mb, 4 * mb:] = -coef

    last_copy.wait_recv()
    first_copy.wait_recv()
    kx_copy.wait_recv()
    for side in range(sides):
        halo_up(side).wait_recv()
        halo_down(side).wait_recv()

    @pl.when(space == n_space - 1)
    def _():
        u_ext[rows + 1] = jnp.zeros((mb, ny), jnp.bfloat16)
        for side in range(sides):
            v_ext[side, rows + 1] = jnp.zeros((mb, ny), jnp.bfloat16)

    pair = pair_ref[...]

    def stack(e, cols):
        u = u_ext[e, :, cols]
        vs = [v_ext[side, e, :, cols] for side in range(sides)]
        return [u, u, vs[0], vs[-1]]

    def weighted(diff, weight_of):
        total = None
        for k in range(terms):
            part = weight_of(k) * diff[k * mb:(k + 1) * mb]
            total = part if total is None else total + part
        return total

    def flux_x(e, cols, weight_of):
        diff = jnp.dot(pair, jnp.concatenate(stack(e + 1, cols) + stack(e, cols), axis=0),
                       preferred_element_type=jnp.float32)
        return weighted(diff, weight_of)

    blocks = [pl.ds(c, LANES) for c in range(0, ny, LANES)]
    keep = jnp.where(space == 0, 0.0, 1.0).astype(jnp.float32)
    for cols in blocks:
        fx_prev[:, cols] = flux_x(0, cols, lambda k: kx_in[k, 7:8, cols]) * keep

    def shifted(x):
        lane = lax.broadcasted_iota(jnp.int32, x.shape, 1)
        moved = pltpu.roll(x.astype(jnp.float32), ny - 1, axis=1)
        return jnp.where(lane == ny - 1, 0.0, moved).astype(jnp.bfloat16)

    def kx_row(r, cols):
        return lambda k: kx_ref[k, pl.ds(r, 1), cols]

    def flux_y_part(r):
        e = r + 1
        sh[0] = shifted(u_ext[e])
        for side in range(sides):
            sh[1 + side] = shifted(v_ext[side, e])
        for cols in blocks:
            ahead = [sh[0, :, cols]] * 2 + [sh[1, :, cols], sh[sides, :, cols]]
            diff = jnp.dot(pair, jnp.concatenate(ahead + stack(e, cols), axis=0),
                           preferred_element_type=jnp.float32)
            fy_row[:, cols] = weighted(diff, lambda k: ky_ref[k, pl.ds(r, 1), cols])
        fy = fy_row[...]
        lane = lax.broadcasted_iota(jnp.int32, fy.shape, 1)
        return jnp.where(lane == 0, 0.0, pltpu.roll(fy, 1, axis=1)) - fy

    def put(r, cols, value):
        for at in range(0, LANES, 128):
            tile = (cols.start + at) // 128
            start = (r // 8) * 8 * (ny // 128) + tile * 8 + r % 8
            out_ref[pl.ds(start, mb, stride=rows * (ny // 128)), :] = value[:, at:at + 128]

    def flux_x_step(r):
        for cols in blocks:
            fx = flux_x(r + 1, cols, kx_row(r, cols))
            put(r, cols, fx_prev[:, cols] - fx + held[:, cols])
            fx_prev[:, cols] = fx

    final = rows - 1
    last_row[...] = flux_y_part(final)
    for cols in blocks:
        last_row[:, cols] = last_row[:, cols] - flux_x(rows, cols, kx_row(final, cols))

    @pl.loop(0, rows - 3)
    def _(r):
        held[...] = flux_y_part(r)
        for side in range(sides):
            row_copy(side, r + 1).wait_recv()
        flux_x_step(r)

    held[...] = flux_y_part(rows - 3)
    for side in range(sides):
        row_copy(side, rows - 2).wait_recv()
    flux_x_step(rows - 3)
    held[...] = flux_y_part(rows - 2)
    flux_x_step(rows - 2)
    for cols in blocks:
        put(final, cols, last_row[:, cols] + fx_prev[:, cols])

    for side in range(sides):
        @pl.loop(0, rows)
        def _(r):
            row_copy(side, r).wait_send()
        halo_up(side).wait_send()
        halo_down(side).wait_send()
    for copy in (coup_copy, last_copy, first_copy, kx_copy):
        copy.wait_send()


def shards(n_mode, n_space, field, kappa_x, kappa_y, coupling, pattern):
    mb, rows, ny = field.shape
    terms = kappa_x.shape[0]
    sides = 1 if n_mode == 2 else 2
    vmem = pl.BlockSpec(memory_space=pltpu.VMEM)
    hbm = pl.BlockSpec(memory_space=pltpu.HBM)
    out = pl.pallas_call(
        functools.partial(kernel, n_mode, n_space),
        out_shape=jax.ShapeDtypeStruct((mb * rows * ny // 128, 128), jnp.float32),
        in_specs=[hbm] * 5,
        out_specs=vmem,
        scratch_shapes=[
            pltpu.VMEM(field.shape, jnp.bfloat16),
            pltpu.VMEM((mb * rows, 128), jnp.float32),
            pltpu.VMEM((rows + 2, mb, ny), jnp.bfloat16),
            pltpu.VMEM((sides, rows + 2, mb, ny), jnp.bfloat16),
            pltpu.VMEM(kappa_x.shape, jnp.float32),
            pltpu.VMEM(kappa_y.shape, jnp.float32),
            pltpu.VMEM(coupling.shape, jnp.bfloat16),
            pltpu.VMEM(pattern.shape, jnp.int32),
            pltpu.VMEM((terms * mb * mb // 128, 128), jnp.bfloat16),
            pltpu.VMEM((terms * mb * mb // 128, 128), jnp.bfloat16),
            pltpu.VMEM((terms * mb, 8 * mb), jnp.bfloat16),
            pltpu.VMEM((terms, 8, ny), jnp.float32),
            pltpu.VMEM((mb, ny), jnp.float32),
            pltpu.VMEM((mb, ny), jnp.float32),
            pltpu.VMEM((mb, ny), jnp.float32),
            pltpu.VMEM((mb, ny), jnp.float32),
            pltpu.VMEM((1 + sides, mb, ny), jnp.bfloat16),
            pltpu.SemaphoreType.DMA((6,)),
            pltpu.SemaphoreType.DMA((sides, rows)),
            pltpu.SemaphoreType.DMA((sides, rows)),
            pltpu.SemaphoreType.DMA((9,)),
            pltpu.SemaphoreType.DMA((9,)),
        ],
        compiler_params=pltpu.CompilerParams(collective_id=0, has_side_effects=True, vmem_limit_bytes=24 * 2**20),
    )(*[pltpu.with_memory_space_constraint(x, pltpu.HBM)
        for x in (field, kappa_x, kappa_y, coupling, pattern)])
    tiles = out.reshape(mb, rows // 8, ny // 128, 8, 128)
    return jnp.swapaxes(tiles, 2, 3).reshape(mb, rows, ny)


def solution(mesh):
    placed = (
        P("mode", "space", None),
        P(None, "space", None),
        P(None, "space", None),
        P("mode", None, None, None),
        P("mode", None, None, None),
    )
    return jax.shard_map(
        functools.partial(shards, mesh.shape["mode"], mesh.shape["space"]),
        mesh=mesh, in_specs=placed, out_specs=P("mode", "space", None), check_vma=False)
```

```python
import functools

import jax
import jax.numpy as jnp
from jax import lax
from jax.experimental import pallas as pl
from jax.experimental.pallas import tpu as pltpu
from jax.sharding import PartitionSpec as P

LANES = 512


def kernel(n_mode, n_space, field_hbm, kx_hbm, ky_hbm, coup_hbm, pat_hbm, out_ref,
           raw, tall, u_ext, v_ext, kx_ref, ky_ref, coup, pat, packed, packed_in, pair_ref,
           kx_in, fx_prev, fy_row, held, last_row, sh,
           local_sem, main_send, main_recv, halo_send, halo_recv):
    mb, rows, ny = field_hbm.shape
    group = 128 // mb
    terms = kx_hbm.shape[0]
    sides = v_ext.shape[0]
    mode = lax.axis_index("mode")
    space = lax.axis_index("space")
    above = {"space": lax.rem(space + 1, n_space)}
    below = {"space": lax.rem(space + n_space - 1, n_space)}
    upper = {"mode": lax.rem(mode + 1, n_mode)}
    lower = {"mode": lax.rem(mode + n_mode - 1, n_mode)}

    barrier = pltpu.get_barrier_semaphore()
    for target in (above, below, upper, lower):
        pl.semaphore_signal(barrier, inc=1, device_id=target, device_id_type=pl.DeviceIdType.MESH)
    locals_ = [
        pltpu.make_async_copy(src, dst, local_sem.at[i])
        for i, (src, dst) in enumerate([
            (field_hbm.at[:, pl.ds(0, 8), :], raw.at[:, pl.ds(0, 8), :]),
            (field_hbm.at[:, pl.ds(8, rows - 8), :], raw.at[:, pl.ds(8, rows - 8), :]),
            (coup_hbm, coup), (pat_hbm, pat), (kx_hbm, kx_ref), (ky_hbm, ky_ref)])]
    for copy in locals_:
        copy.start()

    def masked(slot, k):
        return jnp.where(pat[slot, k] > 0, coup[slot, k].astype(jnp.float32), 0.0)

    def placed(block, shape, offset, flip=False):
        spot = lax.broadcasted_iota(jnp.int32, shape, 0) + offset
        place = jnp.where(lax.broadcasted_iota(jnp.int32, shape, 1) == spot, 1.0, 0.0).astype(jnp.bfloat16)
        return lax.dot_general(block.astype(jnp.bfloat16), place, (((0 if flip else 1,), (0,)), ((), ())),
                               preferred_element_type=jnp.float32)

    def by_rows(first, count):
        for c in range(0, ny, 128):
            tall[:mb * count] = raw[:, first:first + count, c:c + 128].astype(jnp.float32).reshape(mb * count, 128)
            for r in range(count):
                u_ext[first + r + 1, :, c:c + 128] = tall[pl.ds(r, mb, stride=count), :].astype(jnp.bfloat16)

    locals_[0].wait()
    by_rows(0, 8)
    pl.semaphore_wait(barrier, 4)

    def remote(src, dst, send, recv, target):
        return pltpu.make_async_remote_copy(
            src_ref=src, dst_ref=dst, send_sem=send, recv_sem=recv,
            device_id=target, device_id_type=pl.DeviceIdType.MESH)

    towards = (lower, upper)

    def row_copy(side, r):
        return remote(u_ext.at[r + 1], v_ext.at[side, r + 1], main_send.at[side, r], main_recv.at[side, r], towards[side])

    def halo_up(side):
        return remote(v_ext.at[side, rows], v_ext.at[side, 0], halo_send.at[4 + side], halo_recv.at[4 + side], above)

    def halo_down(side):
        return remote(v_ext.at[side, 1], v_ext.at[side, rows + 1], halo_send.at[6 + side], halo_recv.at[6 + side], below)

    coup_copy = remote(packed, packed_in, halo_send.at[0], halo_recv.at[0], upper)
    last_copy = remote(u_ext.at[rows], u_ext.at[0], halo_send.at[1], halo_recv.at[1], above)
    first_copy = remote(u_ext.at[1], u_ext.at[rows + 1], halo_send.at[2], halo_recv.at[2], below)
    kx_copy = remote(kx_hbm.at[:, pl.ds(rows - 8, 8), :], kx_in, halo_send.at[3], halo_recv.at[3], above)

    for side in range(sides):
        row_copy(side, 0).start()
    first_copy.start()
    kx_copy.start()
    locals_[1].wait()
    by_rows(8, rows - 8)
    for side in range(sides):
        row_copy(side, rows - 1).start()
        row_copy(side, 1).start()
        row_copy(side, 2).start()
    last_copy.start()

    locals_[2].wait()
    locals_[3].wait()
    for q in range(terms // group):
        beside = None
        for p in range(group):
            part = placed(masked(1, q * group + p), (mb, 128), p * mb, flip=True)
            beside = part if beside is None else beside + part
        packed[q * mb:(q + 1) * mb] = beside.astype(jnp.bfloat16)

    coup_copy.start()
    for side in range(sides):
        @pl.loop(3, rows - 1)
        def _(r):
            row_copy(side, r).start()

    for side in range(sides):
        row_copy(side, 0).wait_recv()
        halo_down(side).start()
        row_copy(side, rows - 1).wait_recv()
        halo_up(side).start()
    coup_copy.wait_recv()
    for copy in locals_[4:]:
        copy.wait()

    for k in range(terms):
        q, p = divmod(k, group)
        half = masked(0, k) * 0.5
        shape = (mb, 4 * mb)
        coef = (placed(half, shape, 0) + placed(half, shape, mb, flip=True) + placed(masked(1, k), shape, 2 * mb)
                + placed(packed_in[q * mb:(q + 1) * mb, p * mb:(p + 1) * mb], shape, 3 * mb)).astype(jnp.bfloat16)
        pair_ref[k * mb:(k + 1) * mb, :4 * mb] = coef
        pair_ref[k * mb:(k + 1) * mb, 4 * mb:] = -coef

    last_copy.wait_recv()
    first_copy.wait_recv()
    kx_copy.wait_recv()
    for side in range(sides):
        halo_up(side).wait_recv()
        halo_down(side).wait_recv()

    @pl.when(space == n_space - 1)
    def _():
        u_ext[rows + 1] = jnp.zeros((mb, ny), jnp.bfloat16)
        for side in range(sides):
            v_ext[side, rows + 1] = jnp.zeros((mb, ny), jnp.bfloat16)

    pair = pair_ref[...]

    def stack(e, cols):
        u = u_ext[e, :, cols]
        vs = [v_ext[side, e, :, cols] for side in range(sides)]
        return [u, u, vs[0], vs[-1]]

    def weighted(diff, weight_of):
        total = None
        for k in range(terms):
            part = weight_of(k) * diff[k * mb:(k + 1) * mb]
            total = part if total is None else total + part
        return total

    def flux_x(e, cols, weight_of):
        diff = jnp.dot(pair, jnp.concatenate(stack(e + 1, cols) + stack(e, cols), axis=0),
                       preferred_element_type=jnp.float32)
        return weighted(diff, weight_of)

    blocks = [pl.ds(c, LANES) for c in range(0, ny, LANES)]
    keep = jnp.where(space == 0, 0.0, 1.0).astype(jnp.float32)
    for cols in blocks:
        fx_prev[:, cols] = flux_x(0, cols, lambda k: kx_in[k, 7:8, cols]) * keep

    def shifted(x):
        lane = lax.broadcasted_iota(jnp.int32, x.shape, 1)
        moved = pltpu.roll(x.astype(jnp.float32), ny - 1, axis=1)
        return jnp.where(lane == ny - 1, 0.0, moved).astype(jnp.bfloat16)

    def kx_row(r, cols):
        return lambda k: kx_ref[k, pl.ds(r, 1), cols]

    def flux_y_part(r):
        e = r + 1
        sh[0] = shifted(u_ext[e])
        for side in range(sides):
            sh[1 + side] = shifted(v_ext[side, e])
        for cols in blocks:
            ahead = [sh[0, :, cols]] * 2 + [sh[1, :, cols], sh[sides, :, cols]]
            diff = jnp.dot(pair, jnp.concatenate(ahead + stack(e, cols), axis=0),
                           preferred_element_type=jnp.float32)
            fy_row[:, cols] = weighted(diff, lambda k: ky_ref[k, pl.ds(r, 1), cols])
        fy = fy_row[...]
        lane = lax.broadcasted_iota(jnp.int32, fy.shape, 1)
        return jnp.where(lane == 0, 0.0, pltpu.roll(fy, 1, axis=1)) - fy

    def put(r, cols, value):
        for at in range(0, LANES, 128):
            tile = (cols.start + at) // 128
            start = (r // 8) * 8 * (ny // 128) + tile * 8 + r % 8
            out_ref[pl.ds(start, mb, stride=rows * (ny // 128)), :] = value[:, at:at + 128]

    def flux_x_step(r):
        for cols in blocks:
            fx = flux_x(r + 1, cols, kx_row(r, cols))
            put(r, cols, fx_prev[:, cols] - fx + held[:, cols])
            fx_prev[:, cols] = fx

    final = rows - 1
    last_row[...] = flux_y_part(final)
    for cols in blocks:
        last_row[:, cols] = last_row[:, cols] - flux_x(rows, cols, kx_row(final, cols))

    @pl.loop(0, rows - 3)
    def _(r):
        held[...] = flux_y_part(r)
        for side in range(sides):
            row_copy(side, r + 1).wait_recv()
        flux_x_step(r)

    held[...] = flux_y_part(rows - 3)
    for side in range(sides):
        row_copy(side, rows - 2).wait_recv()
    flux_x_step(rows - 3)
    held[...] = flux_y_part(rows - 2)
    flux_x_step(rows - 2)
    for cols in blocks:
        put(final, cols, last_row[:, cols] + fx_prev[:, cols])

    for side in range(sides):
        @pl.loop(0, rows)
        def _(r):
            row_copy(side, r).wait_send()
        halo_up(side).wait_send()
        halo_down(side).wait_send()
    for copy in (coup_copy, last_copy, first_copy, kx_copy):
        copy.wait_send()


def shards(n_mode, n_space, field, kappa_x, kappa_y, coupling, pattern):
    mb, rows, ny = field.shape
    terms = kappa_x.shape[0]
    sides = 1 if n_mode == 2 else 2
    vmem = pl.BlockSpec(memory_space=pltpu.VMEM)
    hbm = pl.BlockSpec(memory_space=pltpu.HBM)
    out = pl.pallas_call(
        functools.partial(kernel, n_mode, n_space),
        out_shape=jax.ShapeDtypeStruct((mb * rows * ny // 128, 128), jnp.float32),
        in_specs=[hbm] * 5,
        out_specs=vmem,
        scratch_shapes=[
            pltpu.VMEM(field.shape, jnp.bfloat16),
            pltpu.VMEM((mb * rows, 128), jnp.float32),
            pltpu.VMEM((rows + 2, mb, ny), jnp.bfloat16),
            pltpu.VMEM((sides, rows + 2, mb, ny), jnp.bfloat16),
            pltpu.VMEM(kappa_x.shape, jnp.float32),
            pltpu.VMEM(kappa_y.shape, jnp.float32),
            pltpu.VMEM(coupling.shape, jnp.bfloat16),
            pltpu.VMEM(pattern.shape, jnp.int32),
            pltpu.VMEM((terms * mb * mb // 128, 128), jnp.bfloat16),
            pltpu.VMEM((terms * mb * mb // 128, 128), jnp.bfloat16),
            pltpu.VMEM((terms * mb, 8 * mb), jnp.bfloat16),
            pltpu.VMEM((terms, 8, ny), jnp.float32),
            pltpu.VMEM((mb, ny), jnp.float32),
            pltpu.VMEM((mb, ny), jnp.float32),
            pltpu.VMEM((mb, ny), jnp.float32),
            pltpu.VMEM((mb, ny), jnp.float32),
            pltpu.VMEM((1 + sides, mb, ny), jnp.bfloat16),
            pltpu.SemaphoreType.DMA((6,)),
            pltpu.SemaphoreType.DMA((sides, rows)),
            pltpu.SemaphoreType.DMA((sides, rows)),
            pltpu.SemaphoreType.DMA((9,)),
            pltpu.SemaphoreType.DMA((9,)),
        ],
        compiler_params=pltpu.CompilerParams(collective_id=0, has_side_effects=True, vmem_limit_bytes=24 * 2**20),
    )(*[pltpu.with_memory_space_constraint(x, pltpu.HBM)
        for x in (field, kappa_x, kappa_y, coupling, pattern)])
    tiles = out.reshape(mb, rows // 8, ny // 128, 8, 128)
    return jnp.swapaxes(tiles, 2, 3).reshape(mb, rows, ny)


def solution(mesh):
    placed = (
        P("mode", "space", None),
        P(None, "space", None),
        P(None, "space", None),
        P("mode", None, None, None),
        P("mode", None, None, None),
    )
    return jax.shard_map(
        functools.partial(shards, mesh.shape["mode"], mesh.shape["space"]),
        mesh=mesh, in_specs=placed, out_specs=P("mode", "space", None), check_vma=False)
```
